128 devices in a mesh: tm: 8 (over y, core), gx: 16 (over x, z).
Axes of the slice: x: 4, y: 4, z: 4, core: 2. Of those that a mesh axis runs over, the one named last changes fastest.
Arguments:
- end_modes: float32 [8, 256, 256, 256], P('tm', None, 'gx'), may hold values from -1 to 1
- initial_modes: float32 [256, 256, 256], P(None, 'gx'), may hold values from -1 to 1
Outputs:
- new_end_modes: float32 [8, 256, 256, 256], P('tm', None, 'gx')
- coarse_ends: float32 [8, 128, 128, 128], P('tm', None, 'gx')
The draws below stay inside these ranges and needn't reach their ends.
All inputs are finite; a program needn't handle non-finite values.
Results may differ from the reference program's by a relative error of at most 0.00014.
Values sent between devices are 32-bit elements; how exact they have to be, the bound alone decides.
A program may use at most 128 MiB of HBM per device.

```python
import math
import jax
import jax.numpy as jnp

GRID = 256
SLICES = 8
N_GX = 16


def draw_end_modes(key, part):
    own_key = jax.random.fold_in(key, 11)
    extent = (SLICES, GRID, GRID, GRID)
    values = jnp.clip(0.25 * jax.random.normal(own_key, extent, jnp.float32), -1.0, 1.0)
    return values


def draw_initial_modes(key, part):
    own_key = jax.random.fold_in(key, 23)
    extent = (GRID, GRID, GRID)
    values = jnp.clip(0.25 * jax.random.normal(own_key, extent, jnp.float32), -1.0, 1.0)
    return values


def setup_inputs(seed: int = 0) -> dict:
    arg_keys = jax.random.split(jax.random.key(seed), 3)
    end_modes = draw_end_modes(jax.random.fold_in(arg_keys[2], 71), 0)
    initial_modes = draw_initial_modes(jax.random.fold_in(arg_keys[2], 71), 0)
    return dict(end_modes=end_modes, initial_modes=initial_modes)


DIFFUSION = 0.25

def sine_axis(field, axis):
    length = field.shape[axis]
    moved = jnp.moveaxis(field, axis, -1)
    zero = jnp.zeros(moved.shape[:-1] + (1,), moved.dtype)
    extended = jnp.concatenate([zero, moved, zero, -moved[..., ::-1]], axis=-1)
    spectrum = jnp.fft.rfft(extended, axis=-1)
    result = -jnp.imag(spectrum[..., 1:length + 1]) * (0.5 * math.sqrt(2.0 / (length + 1)))
    return jnp.moveaxis(result.astype(field.dtype), -1, axis)

def sine_cube(field):
    return sine_axis(sine_axis(sine_axis(field, 0), 1), 2)

def omega(count):
    modes = jnp.arange(count, dtype=jnp.int32).astype(jnp.float32)
    return 2.0 - 2.0 * jnp.cos((modes + 1.0) * (math.pi / (count + 1)))

def reaction(field):
    return field - field * field * field

def reference(end_modes, initial_modes):
    grid = GRID
    coarse = grid // 2
    block = grid // N_GX
    half = block // 2
    positions = jnp.arange(grid, dtype=jnp.int32)
    within = positions % block
    group = positions // block
    mode_of = jnp.where(within < half, group * half + within, coarse + group * half + within - half).astype(jnp.int32)
    lower = positions < coarse
    shifted = jnp.where(lower, positions, positions - coarse)
    position_of = (shifted // half * block + shifted % half + jnp.where(lower, 0, half)).astype(jnp.int32)
    fine_w = omega(grid)
    coarse_w = omega(coarse)
    fine_eigen = DIFFUSION * (fine_w[:, None, None] + fine_w[None, :, None] + fine_w[None, None, :])
    coarse_eigen = 0.25 * DIFFUSION * (coarse_w[:, None, None] + coarse_w[None, :, None] + coarse_w[None, None, :])
    factor = ((coarse + 1) / (grid + 1)) ** 1.5

    def natural(modes):
        return jnp.take(modes, position_of, axis=1)

    def restrict(modes):
        return factor * modes[:coarse, :coarse, :coarse]
    low_eigen = fine_eigen[:coarse, :coarse, :coarse]
    new_list = []
    coarse_list = []
    previous_coarse = None
    for slice_number in range(SLICES):
        if slice_number == 0:
            start_modes = natural(initial_modes)
        else:
            start_modes = natural(end_modes[slice_number - 1])
        start_field = sine_cube(start_modes)
        start_reaction = sine_cube(reaction(start_field))
        node_mid = (start_modes + 0.5 * start_reaction) / (1.0 + 0.5 * fine_eigen)
        node_end = (start_modes + start_reaction) / (1.0 + fine_eigen)
        mid_reaction = restrict(sine_cube(reaction(sine_cube(node_mid))))
        end_reaction = restrict(sine_cube(reaction(sine_cube(node_end))))
        first_term = restrict(start_reaction) - low_eigen * restrict(start_modes)
        mid_term = mid_reaction - low_eigen * restrict(node_mid)
        end_term = end_reaction - low_eigen * restrict(node_end)
        integral = (first_term + 4.0 * mid_term + end_term) / 6.0
        if slice_number == 0:
            coarse_start = restrict(start_modes)
        else:
            coarse_start = previous_coarse
        coarse_end = (coarse_start + integral + coarse_eigen * restrict(node_end)) / (1.0 + coarse_eigen)
        previous_coarse = coarse_end
        corrected = node_end.at[:coarse, :coarse, :coarse].set(coarse_end / factor)
        new_list.append(jnp.take(corrected, mode_of, axis=1))
        coarse_list.append(coarse_end)
    return (jnp.stack(new_list), jnp.stack(coarse_list))
```

```python
import math

import jax
import jax.numpy as jnp
from jax import lax
from jax.sharding import PartitionSpec as P

DIFFUSION = 0.25
HIGH = lax.Precision.HIGH


def sine_table(length, rows, modes):
    phase = (rows[:, None] + 1) * (modes[None, :] + 1) % (2 * (length + 1))
    angle = phase.astype(jnp.float32) * (math.pi / (length + 1))
    return jnp.sin(angle) * math.sqrt(2.0 / (length + 1))


def fine_order(positions, block, coarse):
    within = positions % block
    group = positions // block
    half = block // 2
    return jnp.where(within < half, group * half + within, coarse + group * half + within - half)


def omega(modes, length):
    return 2.0 - 2.0 * jnp.cos((modes.astype(jnp.float32) + 1.0) * (math.pi / (length + 1)))


def reaction(field):
    return field - field * field * field


def slab_solve(right, below, above, diagonal, coupling):
    depth = right.shape[0]
    value, ratio = below, jnp.zeros_like(below)
    values, ratios = [], []
    for i in range(depth):
        scale = 1.0 / (diagonal - coupling * ratio)
        value = (right[i] + coupling * value) * scale
        ratio = coupling * scale
        values.append(value)
        ratios.append(ratio)
    out = [None] * depth
    upper = above
    for i in reversed(range(depth)):
        upper = values[i] + ratios[i] * upper
        out[i] = upper
    return jnp.stack(out)


def per_device(end_modes, initial_modes):
    grid = initial_modes.shape[0]
    coarse = grid // 2
    groups = lax.axis_size("gx")
    slices = lax.axis_size("tm")
    block = grid // groups
    half = block // 2
    slice_index = lax.axis_index("tm")
    group_index = lax.axis_index("gx")
    every = jnp.arange(grid, dtype=jnp.int32)
    order = fine_order(every, block, coarse)
    low = every[:coarse]
    table = sine_table(grid, every, every)
    permuted = sine_table(grid, every, order)
    local_rows = group_index * block + jnp.arange(block, dtype=jnp.int32)
    fine_z = omega(every, grid)
    fine_y = omega(fine_order(local_rows, block, coarse), grid)
    fine_eigen = DIFFUSION * (fine_z[:, None, None] + fine_y[None, :, None] + fine_z[None, None, :])
    plane_eigen = DIFFUSION * (omega(order, grid)[:, None] + fine_z[None, :])
    coarse_z = omega(low, coarse)
    coarse_y = omega(group_index * half + jnp.arange(half, dtype=jnp.int32), coarse)
    coarse_eigen = 0.25 * DIFFUSION * (
        coarse_z[:, None, None] + coarse_y[None, :, None] + coarse_z[None, None, :]
    )
    factor = ((coarse + 1) / (grid + 1)) ** 1.5

    sent = jnp.where(slice_index == slices - 1, initial_modes, end_modes[0])
    start_modes = lax.ppermute(sent, "tm", [(i, (i + 1) % slices) for i in range(slices)])
    spread = jnp.einsum("qz,zpk->qpk", table, start_modes, precision=HIGH)
    start_slab = lax.all_to_all(spread, "gx", split_axis=0, concat_axis=1, tiled=True)
    along = jnp.einsum("yp,zpk->zyk", permuted, start_slab, precision=HIGH)
    field = jnp.einsum("zyk,kx->zyx", along, table, precision=HIGH)
    along = jnp.einsum("zyx,xk->zyk", reaction(field), table, precision=HIGH)
    react_slab = jnp.einsum("yp,zyk->zpk", permuted, along, precision=HIGH)
    react_rows = lax.all_to_all(react_slab, "gx", split_axis=1, concat_axis=0, tiled=True)
    start_reaction = jnp.einsum("qz,zpk->qpk", table, react_rows, precision=HIGH)
    node_mid = (start_modes + 0.5 * start_reaction) / (1.0 + 0.5 * fine_eigen)
    node_end = (start_modes + start_reaction) / (1.0 + fine_eigen)

    edge = jnp.arange(groups, dtype=jnp.int32)[:, None] * block + jnp.array([-1, block], jnp.int32)
    edge = edge.reshape(-1)
    edges = jnp.where((edge < grid)[:, None], sine_table(grid, edge, every), 0.0)
    both = jnp.stack([node_mid, node_end])
    rims = jnp.einsum("ek,nkpx->enpx", edges, both, precision=HIGH)
    rims = lax.all_to_all(rims, "gx", split_axis=0, concat_axis=2, tiled=True)
    mid_slab = slab_solve(
        start_slab + 0.5 * react_slab, rims[0, 0], rims[1, 0],
        1.0 + 0.5 * plane_eigen + DIFFUSION, 0.5 * DIFFUSION,
    )
    end_slab = slab_solve(
        start_slab + react_slab, rims[0, 1], rims[1, 1],
        1.0 + plane_eigen + 2.0 * DIFFUSION, DIFFUSION,
    )

    def planes_back(stack):
        along_y = jnp.einsum("yp,zpk->zyk", permuted, stack, precision=HIGH)
        return jnp.einsum("zyk,kx->zyx", along_y, table, precision=HIGH)

    term = 4.0 * reaction(planes_back(mid_slab)) + reaction(planes_back(end_slab))
    along = jnp.einsum("zyx,xk->zyk", term, table[:, :coarse], precision=HIGH)
    term = jnp.einsum("yp,zyk->zpk", table[:, :coarse], along, precision=HIGH)
    term = lax.all_to_all(term, "gx", split_axis=1, concat_axis=0, tiled=True)
    term = jnp.einsum("qz,zpk->qpk", table[:coarse], term, precision=HIGH)

    def low_of(modes):
        return modes[:coarse, :half, :coarse]

    start_low, mid_low, end_low = low_of(start_modes), low_of(node_mid), low_of(node_end)
    integral = factor / 6.0 * (
        low_of(start_reaction) + term - low_of(fine_eigen) * (start_low + 4.0 * mid_low + end_low)
    )
    decay = 1.0 / (1.0 + coarse_eigen)
    offset = integral + coarse_eigen * (factor * end_low)
    offset = (offset + jnp.where(slice_index == 0, factor * start_low, 0.0)) * decay

    part = coarse // slices
    shared = lax.all_to_all(offset, "tm", split_axis=0, concat_axis=0, tiled=True)
    shared = shared.reshape(slices, part, half, coarse)
    part_decay = lax.dynamic_slice_in_dim(decay, slice_index * part, part, 0)
    current = shared[0]
    ends = [current]
    for n in range(1, slices):
        current = part_decay * current + shared[n]
        ends.append(current)
    ends = jnp.concatenate(ends, axis=0)
    coarse_end = lax.all_to_all(ends, "tm", split_axis=0, concat_axis=0, tiled=True)
    corrected = node_end.at[:coarse, :half, :coarse].set(coarse_end / factor)
    return (corrected[None], coarse_end[None])


def solution(mesh):
    return jax.shard_map(
        per_device,
        mesh=mesh,
        in_specs=(P("tm", None, "gx", None), P(None, "gx", None)),
        out_specs=(P("tm", None, "gx", None), P("tm", None, "gx", None)),
        check_vma=False,
    )
```

```python
import functools
import math

import jax
import jax.numpy as jnp
import ml_dtypes
import numpy as np
from jax import lax
from jax.experimental import pallas as pl
from jax.experimental.pallas import tpu as pltpu
from jax.sharding import PartitionSpec as P

F32, BF16 = jnp.float32, jnp.bfloat16
MESH = pl.DeviceIdType.MESH
GRID, COARSE, GROUPS, SLICES, BLOCK, HALF, LANES = 256, 128, 16, 8, 16, 8, 128
ROUNDS, STEP = 4, 4
DIFFUSION = 0.25
FACTOR = ((COARSE + 1) / (GRID + 1)) ** 1.5
OFFSETS = (10, 9, 11, 6, 14, 2, 8, 5, 7, 13, 15, 1, 3, 4, 12, 0)


def sine_rows(length, rows, modes):
    phase = (rows[:, None] + 1) * (modes[None, :] + 1) % (2 * (length + 1))
    return np.sin(phase * (math.pi / (length + 1))) * math.sqrt(2.0 / (length + 1))


def omega(modes, length):
    return 2.0 - 2.0 * np.cos((modes + 1.0) * (math.pi / (length + 1)))


def two(table):
    high = table.astype(ml_dtypes.bfloat16)
    rest = table - high.astype(np.float64)
    return high, rest.astype(ml_dtypes.bfloat16)


def left(table):
    high, rest = two(table)
    return np.concatenate([high, high, rest], axis=1)


def right(table):
    high, rest = two(table)
    return np.concatenate([high, rest, high], axis=0)


def tables():
    every = np.arange(GRID)
    within, group = every % BLOCK, every // BLOCK
    order = np.where(within < HALF, group * HALF + within, COARSE + group * HALF + within - HALF)
    edge = (np.arange(GROUPS) * BLOCK + np.array([[-1], [BLOCK]])).reshape(-1)
    served = every.reshape(GROUPS, ROUNDS, STEP).transpose(1, 0, 2).reshape(-1)
    edges = np.where((edge < GRID)[:, None], sine_rows(GRID, edge, every), 0.0)
    natural = sine_rows(GRID, every, every)
    permuted = sine_rows(GRID, every, order)
    fine, coarse = omega(every, GRID), omega(np.arange(COARSE), COARSE)
    wide = np.ones((1, LANES))
    as32 = lambda a: np.ascontiguousarray(a, dtype=np.float32)
    return dict(
        nat=left(natural),
        ser=left(natural[served]),
        fan=right(natural),
        per=left(permuted),
        pet=left(permuted.T),
        edg=left(edges),
        col_z=as32(DIFFUSION * fine[:, None] * wide),
        col_p=as32(DIFFUSION * fine[order][:, None] * wide),
        row_x=as32(np.broadcast_to(DIFFUSION * fine.reshape(2, 1, LANES), (2, 8, LANES))),
        col_c=as32(0.25 * DIFFUSION * coarse[:, None] * wide),
        row_c=as32(np.broadcast_to(0.25 * DIFFUSION * coarse[None, :], (8, LANES))),
        sub_c=as32(0.25 * DIFFUSION * coarse.reshape(GROUPS, HALF, 1) * wide),
        scal_p=as32(DIFFUSION * fine[order]),
        scal_c=as32(0.25 * DIFFUSION * coarse),
    )


def split(value):
    high = value.astype(BF16)
    return high, (value - high.astype(F32)).astype(BF16)


def table_times(table, value):
    high, rest = split(value)
    return jnp.dot(table, jnp.concatenate([high, rest, high], axis=0), preferred_element_type=F32)


def times_table(value, table):
    high, rest = split(value)
    return jnp.dot(jnp.concatenate([high, high, rest], axis=1), table, preferred_element_type=F32)


def reaction(field):
    return field - field * field * field


def kernel(
    end_hbm, initial_hbm, nat, ser, fan, per, pet, edg, col_z, col_p, row_x, col_c, row_c, sub_c, scal_p, scal_c,
    new, coarse,
    s_in, spread, slab, react, own, phi, base, rim_out, rim, mix_out, mix, low, low_in, ends, coarse_own, low_out,
    load_sem, in_send, in_recv, r_send, r_recv, b_send, b_recv, n_send, n_recv, l_send, l_recv,
    m_send, m_recv, e_send, e_recv, ready,
):
    t, g = lax.axis_index("tm"), lax.axis_index("gx")
    after = lax.rem(t + 1, SLICES)

    g_x, g_z = g // 4, g % 4
    along_x, along_plane = [(g_x + i) % 4 * 4 for i in range(4)], [(g_z + i) % 4 for i in range(4)]
    partners = [along_x[k // 4] + along_plane[k % 4] for k in range(GROUPS)]
    others = [lax.rem(t + k, SLICES) for k in range(SLICES)]

    def partner(k):
        return partners[k]

    def load(source, h):
        return pltpu.make_async_copy(source.at[:, :, pl.ds(h * LANES, LANES)], s_in.at[h], load_sem.at[h])

    @pl.when(t == SLICES - 1)
    def _():
        for h in range(2):
            load(initial_hbm, h).start()

    @pl.when(t != SLICES - 1)
    def _():
        for h in range(2):
            load(end_hbm.at[0], h).start()

    barrier = pltpu.get_barrier_semaphore()

    def greet(device):
        pl.semaphore_signal(barrier, inc=1, device_id=device, device_id_type=MESH)

    for k in range(1, GROUPS):
        greet((t, partner(k)))
    for k in range(1, SLICES):
        greet((others[k], g))

    def whole(plane):
        return plane.reshape(GRID, LANES)

    def two_rows(ref, y, stride):
        return jnp.concatenate([ref[pl.ds(y + i, GRID, stride=stride), :] for i in range(2)], axis=1)

    def halves(value):
        return value[:, :LANES], value[:, LANES:]

    s_rows = s_in.reshape(2, GRID * BLOCK, LANES)
    spread_rows = spread.reshape(2, GRID * BLOCK, LANES)
    own_rows = pl.multiple_of(g * BLOCK, BLOCK)

    def along_z(h, first, last):
        start, count = first * GRID // ROUNDS, (last - first) * GRID // ROUNDS

        def body(j, carry):
            value = table_times(ser[start : start + count, :], two_rows(s_rows.at[h], 2 * j, BLOCK))
            for i, half in enumerate(halves(value)):
                spread_rows[h, pl.ds(start * BLOCK + 2 * j + i, count, stride=BLOCK), :] = half
            return carry

        lax.fori_loop(0, BLOCK // 2, body, 0)

    def send_start(r, lanes):
        for k in OFFSETS[:-1]:
            to = partner(k)
            pltpu.make_async_remote_copy(
                src_ref=spread.at[lanes, r, to],
                dst_ref=slab.at[lanes, g, pl.ds(r * STEP, STEP)],
                send_sem=in_send,
                recv_sem=in_recv.at[r],
                device_id=(t, to),
                device_id_type=MESH,
            ).start()
        pltpu.make_async_copy(
            spread.at[lanes, r, g], slab.at[lanes, g, pl.ds(r * STEP, STEP)], in_recv.at[r]
        ).start()

    with jax.named_scope("ph_along0"):
        load(initial_hbm, 0).wait()
        along_z(0, 0, 1)
    with jax.named_scope("ph_barrier"):
        pl.semaphore_wait(barrier, GROUPS + SLICES - 2)
    send_start(0, pl.ds(0, 1))
    with jax.named_scope("ph_along1"):
        load(initial_hbm, 1).wait()
        along_z(1, 0, 1)
    send_start(0, pl.ds(1, 1))
    for k in range(1, SLICES):
        pl.semaphore_signal(ready, inc=1, device_id=(others[k], g), device_id_type=MESH)
    with jax.named_scope("ph_along2"):
        for h in range(2):
            along_z(h, 1, ROUNDS)
    for r in range(1, ROUNDS):
        send_start(r, pl.ds(0, 2))
    pieces = [(h, q) for h in range(2) for q in range(2)]

    couplings = (0.5 * DIFFUSION, DIFFUSION)

    def diagonal(n, octet, h):
        plane = col_p[pl.ds(octet, 8), :] + row_x[h]
        return 1.0 + 0.5 * plane + DIFFUSION if n == 0 else 1.0 + plane + 2.0 * DIFFUSION

    def ratios(n, octet, h):
        d, b = diagonal(n, octet, h), couplings[n]
        out = [b / d]
        for _ in range(BLOCK - 1):
            out.append(b / (d - b * out[-1]))
        return out

    def unit(o, carry):
        octet = pl.multiple_of(o * 8, 8)
        for n in range(2):
            for h in range(2):
                c = ratios(n, octet, h)
                v = [c[0]]
                for i in range(1, BLOCK):
                    v.append(c[i] * v[-1])
                upper = v[-1]
                phi[n, h, BLOCK - 1, pl.ds(octet, 8), :] = upper
                for i in reversed(range(BLOCK - 1)):
                    upper = v[i] + c[i] * upper
                    phi[n, h, i, pl.ds(octet, 8), :] = upper
        return carry

    with jax.named_scope("ph_unit"):
        lax.fori_loop(0, GRID // 8, unit, 0)

    def send_react(p, start, count):
        h, q = pieces[p]
        planes, places = pl.ds(start, count), pl.ds(own_rows + start, count)
        for k in OFFSETS[:-1]:
            to = partner(k)
            pltpu.make_async_remote_copy(
                src_ref=react.at[h, q, to, planes],
                dst_ref=own.at[h, q, places],
                send_sem=r_send, recv_sem=r_recv.at[p], device_id=(t, to), device_id_type=MESH,
            ).start()
        pltpu.make_async_copy(react.at[h, q, g, planes], own.at[h, q, places], r_recv.at[p]).start()

    def start_planes(j, carry):
        planes = (2 * j, 2 * j + 1)
        values = [jnp.concatenate([whole(slab[h, :, z]) for h in range(2)], axis=1) for z in planes]
        values = [table_times(per[...], value) for value in values]
        values = [reaction(times_table(value, fan[...])) for value in values]
        values = [times_table(value, fan[...]) for value in values]
        values = [table_times(pet[...], value) for value in values]
        for z, value in zip(planes, values):
            for h, half in enumerate(halves(value)):
                half = half.reshape(GROUPS, 2, 8, LANES)
                for q in range(2):
                    react[h, q, :, z] = half[:, q]
        return carry

    for r in range(ROUNDS):
        arrived = slab.at[:, :, pl.ds(r * STEP, STEP)]
        with jax.named_scope(f"ph_wait_in{r}"):
            pltpu.make_async_copy(arrived, arrived, in_recv.at[r]).wait()
        with jax.named_scope(f"ph_start{r}"):
            lax.fori_loop(r * STEP // 2, (r + 1) * STEP // 2, start_planes, 0)
        send_react(0, r * STEP, STEP)
    send_react(1, 0, BLOCK)

    def local(o, carry):
        octet = pl.multiple_of(o * 8, 8)
        here = pl.ds(octet, 8)
        for n in range(2):
            for h in range(2):
                c = ratios(n, octet, h)
                v = []
                for i in range(BLOCK):
                    right = slab[h, o // 2, i, pl.ds(o % 2 * 8, 8), :]
                    right = right + (0.5 if n == 0 else 1.0) * react[h, o % 2, o // 2, i]
                    right = right * (1.0 / couplings[n])
                    v.append(c[i] * (right + v[-1] if v else right))
                upper = v[-1]
                base[n, h, BLOCK - 1, here, :] = upper
                for i in reversed(range(BLOCK - 1)):
                    upper = v[i] + c[i] * upper
                    base[n, h, i, here, :] = upper
        return carry

    with jax.named_scope("ph_local"):
        lax.fori_loop(0, GRID // 8, local, 0)

    own_flat = own.reshape(2, 2, GRID * 8, LANES)
    rim_rows = rim_out.reshape(2, 2, GROUPS * 32, LANES)
    first = jnp.where(after == 0, FACTOR, 0.0).astype(F32)
    def in_modes(h, q, y, keep_low):
        start = two_rows(s_rows.at[h], q * 8 + y, BLOCK)
        rate = table_times(nat[...], two_rows(own_flat.at[h, q], y, 8))
        lam = jnp.concatenate(
            [col_z[...] + (row_x[h, :1, :] + scal_p[own_rows + q * 8 + y + i]) for i in range(2)], axis=1
        )
        mid = (start + 0.5 * rate) / (1.0 + 0.5 * lam)
        end = (start + rate) / (1.0 + lam)
        for i, half in enumerate(halves(end)):
            own_flat[h, q, pl.ds(y + i, GRID, stride=8), :] = half
        for n, node in enumerate((mid, end)):
            for i, half in enumerate(halves(table_times(edg[...], node))):
                for side in range(2):
                    place = pl.ds(n * 16 + side * 8 + y + i, GROUPS, stride=32)
                    rim_rows[h, q, place, :] = half[side * GROUPS : (side + 1) * GROUPS]
        if keep_low:
            for i in range(2):
                cut = lambda a: halves(a)[i][:COARSE]
                s_cut, end_cut = cut(start), cut(end)
                lam_c = col_c[...] + (row_c[:1, :] + scal_c[g * HALF + y + i])
                value = (FACTOR / 6.0) * (cut(rate) - cut(lam) * (s_cut + 4.0 * cut(mid) + end_cut))
                low[y + i] = value + lam_c * (FACTOR * end_cut) + first * s_cut

    def hand_on(p):
        h, q = pieces[p]
        kept, piece = pl.ds(COARSE, COARSE) if p == 0 else pl.ds(0, GRID), pl.ds(q * 8, 8)
        return pltpu.make_async_remote_copy(
            src_ref=own.at[h, q, kept],
            dst_ref=new.at[0, kept, piece, pl.ds(h * LANES, LANES)],
            send_sem=n_send.at[p], recv_sem=n_recv.at[p], device_id=(after, g), device_id_type=MESH,
        )

    def modes_of(p):
        h, q = pieces[p]
        here = own.at[h, q]
        with jax.named_scope(f"ph_wait_r{p}"):
            pltpu.make_async_copy(here, here, r_recv.at[p]).wait()

        def body(j, carry):
            in_modes(h, q, 2 * j, p == 0)
            return carry

        with jax.named_scope(f"ph_modes{p}"):
            lax.fori_loop(0, 4, body, 0)
        if p + 2 < len(pieces):
            send_react(p + 2, 0, BLOCK)
        for k in OFFSETS[:-1]:
            to = partner(k)
            pltpu.make_async_remote_copy(
                src_ref=rim_out.at[h, q, to],
                dst_ref=rim.at[h, g, q],
                send_sem=b_send, recv_sem=b_recv.at[h], device_id=(t, to), device_id_type=MESH,
            ).start()
        pltpu.make_async_copy(rim_out.at[h, q, g], rim.at[h, g, q], b_recv.at[h]).start()
        hand_on(p).start()
        if p == 0:
            for k in range(1, SLICES):
                to = lax.rem(t + k, SLICES)
                pltpu.make_async_remote_copy(
                    src_ref=low.at[to], dst_ref=low_in.at[after], send_sem=l_send, recv_sem=l_recv,
                    device_id=(to, g), device_id_type=MESH,
                ).start()
            pltpu.make_async_copy(low.at[t], low_in.at[after], l_recv).start()

    def nodes_on(h, z):
        return jnp.concatenate(
            [
                base[n, h, z]
                + phi[n, h, z] * whole(rim[h, :, :, n, 0])
                + phi[n, h, BLOCK - 1 - z] * whole(rim[h, :, :, n, 1])
                for n in range(2)
            ],
            axis=1,
        )

    def early(j, carry):
        for z in (2 * j, 2 * j + 1):
            for n, half in enumerate(halves(table_times(per[...], nodes_on(0, z)))):
                base[n, 0, z] = half
        return carry

    mix_rows = mix_out.reshape(COARSE * BLOCK, LANES)

    def node_planes(j, carry):
        planes = (2 * j, 2 * j + 1)
        values = [halves(table_times(per[...], nodes_on(1, z))) for z in planes]
        values = [
            [jnp.concatenate([base[n, 0, z], value[n]], axis=1) for n in range(2)]
            for z, value in zip(planes, values)
        ]
        values = [[reaction(times_table(node, fan[...])) for node in value] for value in values]
        values = [times_table(4.0 * value[0] + value[1], fan[:, :COARSE]) for value in values]
        value = table_times(nat[:COARSE, :], jnp.concatenate(values, axis=1))
        for z, half in zip(planes, halves(value)):
            mix_rows[pl.ds(z, COARSE, stride=BLOCK), :] = half
        return carry

    def rim_arrived(h):
        with jax.named_scope(f"ph_wait_rim{h}"):
            pltpu.make_async_copy(rim.at[h], rim.at[h], b_recv.at[h]).wait()

    modes_of(0)
    modes_of(1)
    modes_of(2)
    modes_of(3)
    rim_arrived(0)
    with jax.named_scope("ph_early"):
        lax.fori_loop(0, BLOCK // 2, early, 0)
    rim_arrived(1)

    def mix_source(to_t, to_g, planes):
        return mix_out.at[to_g * HALF + to_t, planes]

    def mix_place(start, count):
        return mix.at[after, pl.ds(pl.multiple_of(own_rows + start, STEP), count)]

    def send_mix(start, count, to_t, k):
        to_g = partner(k)
        pltpu.make_async_remote_copy(
            src_ref=mix_source(to_t, to_g, pl.ds(start, count)), dst_ref=mix_place(start, count),
            send_sem=m_send, recv_sem=m_recv, device_id=(to_t, to_g), device_id_type=MESH,
        ).start()

    def send_rows(start, count, first, last):
        def body(i, carry):
            to_t = lax.rem(t + i, SLICES)
            for k in OFFSETS[:-1]:
                send_mix(start, count, to_t, k)
            return carry

        lax.fori_loop(first, last, body, 0)

    def send_column(start, count):
        pltpu.make_async_copy(mix_source(t, g, pl.ds(start, count)), mix_place(start, count), m_recv).start()
        for i in range(1, SLICES):
            send_mix(start, count, others[i], 0)

    with jax.named_scope("ph_node0"):
        lax.fori_loop(0, 4, node_planes, 0)
    pl.semaphore_wait(ready, SLICES - 1)
    send_column(0, 8)
    send_rows(0, 8, 0, SLICES)

    def node_round(r, carry):
        lax.fori_loop(4 + 2 * r, 6 + 2 * r, node_planes, 0)
        start = pl.multiple_of(8 + STEP * r, STEP)
        send_column(start, STEP)
        send_rows(start, STEP, 0, SLICES)
        return carry

    with jax.named_scope("ph_node1"):
        lax.fori_loop(0, 2, node_round, 0)
    with jax.named_scope("ph_wait_mix"):
        pltpu.make_async_copy(low_in, low_in, l_recv).wait()
        pltpu.make_async_copy(mix, mix, m_recv).wait()

    with jax.named_scope("ph_scan"):
        decay = 1.0 / (1.0 + (col_c[...] + (row_c[:1, :] + scal_c[g * HALF + t])))
        current = None
        for i in range(SLICES // 2):
            value = table_times(nat[:COARSE, :], jnp.concatenate([mix[2 * i], mix[2 * i + 1]], axis=1))
            for n, half in zip((2 * i, 2 * i + 1), halves(value)):
                gain = low_in[n] + (FACTOR / 6.0) * half
                current = decay * (gain if current is None else current + gain)
                ends[n] = current
    for k in range(1, SLICES):
        to = lax.rem(t + k, SLICES)
        pltpu.make_async_remote_copy(
            src_ref=ends.at[to], dst_ref=coarse_own.at[t], send_sem=e_send, recv_sem=e_recv,
            device_id=(to, g), device_id_type=MESH,
        ).start()
    pltpu.make_async_copy(ends.at[t], coarse_own.at[t], e_recv).start()
    with jax.named_scope("ph_wait_e"):
        pltpu.make_async_copy(coarse_own, coarse_own, e_recv).wait()

    coarse_rows = coarse.reshape(COARSE * HALF, LANES)
    low_rows = low_out.reshape(COARSE * HALF, LANES)
    for j in range(HALF):
        coarse_rows[pl.ds(j, COARSE, stride=HALF), :] = coarse_own[j]
        low_rows[pl.ds(j, COARSE, stride=HALF), :] = coarse_own[j] * (1.0 / FACTOR)
    new[0, :COARSE, :HALF, :LANES] = low_out[...]

    def sent(ref, sem):
        pltpu.make_async_copy(ref, ref, sem).wait()

    with jax.named_scope("ph_drain"):
        sent(spread.at[:, :, pl.ds(0, GROUPS - 1)], in_send)
        sent(react.at[:, :, pl.ds(0, GROUPS - 1)], r_send)
        sent(rim_out.at[:, :, pl.ds(0, GROUPS - 1)], b_send)
        sent(low.at[pl.ds(0, SLICES - 1)], l_send)
        sent(mix_out.at[pl.ds(0, COARSE - 1)], m_send)
        sent(ends.at[pl.ds(0, SLICES - 1)], e_send)
        for p in range(len(pieces)):
            hand_on(p).wait()


def solution(mesh):
    vmem = pl.BlockSpec(memory_space=pltpu.VMEM)
    hbm = pl.BlockSpec(memory_space=pl.ANY)
    smem = pl.BlockSpec(memory_space=pltpu.SMEM)
    held = tables()

    def per_device(end_modes, initial_modes):
        slab = (2, BLOCK, GRID, LANES)
        coarse = (COARSE, HALF, LANES)
        share = (SLICES, COARSE, LANES)
        dma = pltpu.SemaphoreType.DMA
        scratch = [
            (2, GRID, BLOCK, LANES), (2, ROUNDS, GROUPS, STEP, BLOCK, LANES), (2, GROUPS, BLOCK, BLOCK, LANES),
            (2, 2, GROUPS, BLOCK, 8, LANES), (2, 2, GRID, 8, LANES), (2, *slab), (2, *slab),
            (2, 2, GROUPS, 2, 2, 8, LANES), (2, GROUPS, 2, 2, 2, 8, LANES),
            (COARSE, BLOCK, LANES), (SLICES, GRID, LANES), share, share, share, share, coarse,
        ]
        counts = [2, 0, ROUNDS, 0, 4, 0, 2, 4, 4, 0, 0, 0, 0, 0, 0]
        sems = [dma((n,)) if n else dma for n in counts] + [pltpu.SemaphoreType.REGULAR]
        return pl.pallas_call(
            kernel,
            name="pfasst",
            out_shape=(
                pltpu.VMEM(end_modes.shape, F32),
                pltpu.VMEM((1, *coarse), F32),
            ),
            in_specs=[hbm, hbm] + [vmem] * 12 + [smem] * 2,
            out_specs=(vmem, vmem),
            scratch_shapes=[pltpu.VMEM(s, F32) for s in scratch] + sems,
            compiler_params=pltpu.CompilerParams(collective_id=0, has_side_effects=True, vmem_limit_bytes=54 << 20),
        )(end_modes, initial_modes, *held.values())

    return jax.shard_map(
        per_device,
        mesh=mesh,
        in_specs=(P("tm", None, "gx", None), P(None, "gx", None)),
        out_specs=(P("tm", None, "gx", None), P("tm", None, "gx", None)),
        check_vma=False,
    )
```

```python
import functools
import math

import jax
import jax.numpy as jnp
import ml_dtypes
import numpy as np
from jax import lax
from jax.experimental import pallas as pl
from jax.experimental.pallas import tpu as pltpu
from jax.sharding import PartitionSpec as P

F32, BF16 = jnp.float32, jnp.bfloat16
MESH = pl.DeviceIdType.MESH
GRID, COARSE, GROUPS, SLICES, BLOCK, HALF, LANES = 256, 128, 16, 8, 16, 8, 128
ROUNDS, STEP = 4, 4
DIFFUSION = 0.25
FACTOR = ((COARSE + 1) / (GRID + 1)) ** 1.5
OFFSETS = (10, 9, 11, 6, 14, 2, 8, 5, 7, 13, 15, 1, 3, 4, 12, 0)


FAR_FIRST = (4, 3, 5, 2, 6, 1, 7)


def sine_rows(length, rows, modes):
    phase = (rows[:, None] + 1) * (modes[None, :] + 1) % (2 * (length + 1))
    return np.sin(phase * (math.pi / (length + 1))) * math.sqrt(2.0 / (length + 1))


def omega(modes, length):
    return 2.0 - 2.0 * np.cos((modes + 1.0) * (math.pi / (length + 1)))


def two(table):
    high = table.astype(ml_dtypes.bfloat16)
    rest = table - high.astype(np.float64)
    return high, rest.astype(ml_dtypes.bfloat16)


def left(table):
    high, rest = two(table)
    return np.concatenate([high, high, rest], axis=1)


def right(table):
    high, rest = two(table)
    return np.concatenate([high, rest, high], axis=0)


def tables():
    every = np.arange(GRID)
    within, group = every % BLOCK, every // BLOCK
    order = np.where(within < HALF, group * HALF + within, COARSE + group * HALF + within - HALF)
    edge = (np.arange(GROUPS) * BLOCK + np.array([[-1], [BLOCK]])).reshape(-1)
    served = every.reshape(GROUPS, ROUNDS, STEP).transpose(1, 0, 2).reshape(-1)
    edges = np.where((edge < GRID)[:, None], sine_rows(GRID, edge, every), 0.0)
    natural = sine_rows(GRID, every, every)
    permuted = sine_rows(GRID, every, order)
    fine, coarse = omega(every, GRID), omega(np.arange(COARSE), COARSE)
    wide = np.ones((1, LANES))
    as32 = lambda a: np.ascontiguousarray(a, dtype=np.float32)
    return dict(
        nat=left(natural),
        ser=left(natural[served]),
        fan=right(natural),
        per=left(permuted),
        pet=left(permuted.T),
        edg=left(edges),
        col_z=as32(DIFFUSION * fine[:, None] * wide),
        col_p=as32(DIFFUSION * fine[order][:, None] * wide),
        row_x=as32(np.broadcast_to(DIFFUSION * fine.reshape(2, 1, LANES), (2, 8, LANES))),
        col_c=as32(0.25 * DIFFUSION * coarse[:, None] * wide),
        row_c=as32(np.broadcast_to(0.25 * DIFFUSION * coarse[None, :], (8, LANES))),
        sub_c=as32(0.25 * DIFFUSION * coarse.reshape(GROUPS, HALF, 1) * wide),
        scal_p=as32(DIFFUSION * fine[order]),
        scal_c=as32(0.25 * DIFFUSION * coarse),
    )


def split(value):
    high = value.astype(BF16)
    return high, (value - high.astype(F32)).astype(BF16)


def table_times(table, value):
    high, rest = split(value)
    return jnp.dot(table, jnp.concatenate([high, rest, high], axis=0), preferred_element_type=F32)


def times_table(value, table):
    high, rest = split(value)
    return jnp.dot(jnp.concatenate([high, high, rest], axis=1), table, preferred_element_type=F32)


def reaction(field):
    return field - field * field * field


def kernel(
    end_hbm, initial_hbm, nat, ser, fan, per, pet, edg, col_z, col_p, row_x, col_c, row_c, sub_c, scal_p, scal_c,
    new, coarse,
    s_in, spread, slab, react, own, phi, base, rim_out, rim, mix_out, mix, low, low_in, ends, coarse_own, low_out, inverse,
    load_sem, in_send, in_recv, r_send, r_recv, b_send, b_recv, n_send, n_recv, l_send, l_recv,
    m_send, m_recv, e_send, e_recv, ready,
):
    t, g = lax.axis_index("tm"), lax.axis_index("gx")
    after = lax.rem(t + 1, SLICES)

    g_x, g_z = g // 4, g % 4
    along_x, along_plane = [(g_x + i) % 4 * 4 for i in range(4)], [(g_z + i) % 4 for i in range(4)]
    partners = [along_x[k // 4] + along_plane[k % 4] for k in range(GROUPS)]
    others = [lax.rem(t + k, SLICES) for k in range(SLICES)]

    def partner(k):
        return partners[k]

    def load(source, h):
        return pltpu.make_async_copy(source.at[:, :, pl.ds(h * LANES, LANES)], s_in.at[h], load_sem.at[h])

    def start_load(h):
        @pl.when(t == SLICES - 1)
        def _():
            load(initial_hbm, h).start()

        @pl.when(t != SLICES - 1)
        def _():
            load(end_hbm.at[0], h).start()

    start_load(0)

    barrier = pltpu.get_barrier_semaphore()

    def greet(device):
        pl.semaphore_signal(barrier, inc=1, device_id=device, device_id_type=MESH)

    for k in range(1, GROUPS):
        greet((t, partner(k)))
    for k in range(1, SLICES):
        greet((others[k], g))

    def whole(plane):
        return plane.reshape(GRID, LANES)

    def two_rows(ref, y, stride):
        return jnp.concatenate([ref[pl.ds(y + i, GRID, stride=stride), :] for i in range(2)], axis=1)

    def halves(value):
        return value[:, :LANES], value[:, LANES:]

    s_rows = s_in.reshape(2, GRID * BLOCK, LANES)
    spread_rows = spread.reshape(2, GRID * BLOCK, LANES)
    own_rows = pl.multiple_of(g * BLOCK, BLOCK)

    def along_z(h, first, last):
        start, count = first * GRID // ROUNDS, (last - first) * GRID // ROUNDS

        def body(j, carry):
            value = table_times(ser[start : start + count, :], two_rows(s_rows.at[h], 2 * j, BLOCK))
            for i, half in enumerate(halves(value)):
                spread_rows[h, pl.ds(start * BLOCK + 2 * j + i, count, stride=BLOCK), :] = half
            return carry

        lax.fori_loop(0, BLOCK // 2, body, 0)

    def send_start(r, lanes):
        for k in OFFSETS[:-1]:
            to = partner(k)
            pltpu.make_async_remote_copy(
                src_ref=spread.at[lanes, r, to],
                dst_ref=slab.at[lanes, g, pl.ds(r * STEP, STEP)],
                send_sem=in_send,
                recv_sem=in_recv.at[r],
                device_id=(t, to),
                device_id_type=MESH,
            ).start()
        pltpu.make_async_copy(
            spread.at[lanes, r, g], slab.at[lanes, g, pl.ds(r * STEP, STEP)], in_recv.at[r]
        ).start()

    with jax.named_scope("ph_along0"):
        load(initial_hbm, 0).wait()
        start_load(1)
        along_z(0, 0, 1)
    with jax.named_scope("ph_barrier"):
        pl.semaphore_wait(barrier, GROUPS + SLICES - 2)
    send_start(0, pl.ds(0, 1))
    with jax.named_scope("ph_along1"):
        load(initial_hbm, 1).wait()
        along_z(1, 0, 1)
    send_start(0, pl.ds(1, 1))
    for k in range(1, SLICES):
        pl.semaphore_signal(ready, inc=1, device_id=(others[k], g), device_id_type=MESH)
    with jax.named_scope("ph_along2"):
        for h in range(2):
            along_z(h, 1, ROUNDS)
    for r in range(1, ROUNDS):
        send_start(r, pl.ds(0, 2))
    pieces = [(h, q) for h in range(2) for q in range(2)]

    couplings = (0.5 * DIFFUSION, DIFFUSION)

    def diagonal(n, octet, h):
        plane = col_p[pl.ds(octet, 8), :] + row_x[h]
        return 1.0 + 0.5 * plane + DIFFUSION if n == 0 else 1.0 + plane + 2.0 * DIFFUSION

    def ratios(n, octet, h):
        d, b = diagonal(n, octet, h), couplings[n]
        out = [b / d]
        for _ in range(BLOCK - 1):
            out.append(b / (d - b * out[-1]))
        return out

    def unit(o, carry):
        octet = pl.multiple_of(o * 8, 8)
        for n in range(2):
            for h in range(2):
                c = ratios(n, octet, h)
                v = [c[0]]
                for i in range(1, BLOCK):
                    v.append(c[i] * v[-1])
                upper = v[-1]
                phi[n, h, BLOCK - 1, pl.ds(octet, 8), :] = upper
                for i in reversed(range(BLOCK - 1)):
                    upper = v[i] + c[i] * upper
                    phi[n, h, i, pl.ds(octet, 8), :] = upper
        return carry

    with jax.named_scope("ph_unit"):
        lax.fori_loop(0, GRID // 8, unit, 0)

    def send_react(p, start, count):
        h, q = pieces[p]
        planes, places = pl.ds(start, count), pl.ds(own_rows + start, count)
        for k in OFFSETS[:-1]:
            to = partner(k)
            pltpu.make_async_remote_copy(
                src_ref=react.at[h, q, to, planes],
                dst_ref=own.at[h, q, places],
                send_sem=r_send, recv_sem=r_recv.at[p], device_id=(t, to), device_id_type=MESH,
            ).start()
        pltpu.make_async_copy(react.at[h, q, g, planes], own.at[h, q, places], r_recv.at[p]).start()

    def start_planes(j, carry):
        planes = (2 * j, 2 * j + 1)
        values = [jnp.concatenate([whole(slab[h, :, z]) for h in range(2)], axis=1) for z in planes]
        values = [table_times(per[...], value) for value in values]
        values = [reaction(times_table(value, fan[...])) for value in values]
        values = [times_table(value, fan[...]) for value in values]
        values = [table_times(pet[...], value) for value in values]
        for z, value in zip(planes, values):
            for h, half in enumerate(halves(value)):
                half = half.reshape(GROUPS, 2, 8, LANES)
                for q in range(2):
                    react[h, q, :, z] = half[:, q]
        return carry

    for r in range(ROUNDS):
        arrived = slab.at[:, :, pl.ds(r * STEP, STEP)]
        with jax.named_scope(f"ph_wait_in{r}"):
            pltpu.make_async_copy(arrived, arrived, in_recv.at[r]).wait()
        with jax.named_scope(f"ph_start{r}"):
            lax.fori_loop(r * STEP // 2, (r + 1) * STEP // 2, start_planes, 0)
        send_react(0, r * STEP, STEP)
    send_react(1, 0, BLOCK)

    def local(o, carry):
        octet = pl.multiple_of(o * 8, 8)
        here = pl.ds(octet, 8)
        for n in range(2):
            for h in range(2):
                c = ratios(n, octet, h)
                v = []
                for i in range(BLOCK):
                    right = slab[h, o // 2, i, pl.ds(o % 2 * 8, 8), :]
                    right = right + (0.5 if n == 0 else 1.0) * react[h, o % 2, o // 2, i]
                    right = right * (1.0 / couplings[n])
                    v.append(c[i] * (right + v[-1] if v else right))
                upper = v[-1]
                base[n, h, BLOCK - 1, here, :] = upper
                for i in reversed(range(BLOCK - 1)):
                    upper = v[i] + c[i] * upper
                    base[n, h, i, here, :] = upper
        return carry

    with jax.named_scope("ph_local"):
        lax.fori_loop(0, GRID // 8, local, 0)

    own_flat = own.reshape(2, 2, GRID * 8, LANES)
    rim_rows = rim_out.reshape(2, 2, GROUPS * 32, LANES)
    first = jnp.where(after == 0, FACTOR, 0.0).astype(F32)
    def eigen(h, q, y):
        return jnp.concatenate(
            [col_z[...] + (row_x[h, :1, :] + scal_p[own_rows + q * 8 + y + i]) for i in range(2)], axis=1
        )

    def in_modes(h, q, y, keep_low):
        start = two_rows(s_rows.at[h], q * 8 + y, BLOCK)
        rate = table_times(nat[...], two_rows(own_flat.at[h, q], y, 8))
        mid = (start + 0.5 * rate) * inverse[0, y // 2]
        end = (start + rate) * inverse[1, y // 2]
        for i, half in enumerate(halves(end)):
            own_flat[h, q, pl.ds(y + i, GRID, stride=8), :] = half
        for n, node in enumerate((mid, end)):
            for i, half in enumerate(halves(table_times(edg[...], node))):
                for side in range(2):
                    place = pl.ds(n * 16 + side * 8 + y + i, GROUPS, stride=32)
                    rim_rows[h, q, place, :] = half[side * GROUPS : (side + 1) * GROUPS]
        if keep_low:
            lam = eigen(h, q, y)
            for i in range(2):
                cut = lambda a: halves(a)[i][:COARSE]
                s_cut, end_cut = cut(start), cut(end)
                lam_c = col_c[...] + (row_c[:1, :] + scal_c[g * HALF + y + i])
                value = (FACTOR / 6.0) * (cut(rate) - cut(lam) * (s_cut + 4.0 * cut(mid) + end_cut))
                low[y + i] = value + lam_c * (FACTOR * end_cut) + first * s_cut

    def hand_on(p):
        h, q = pieces[p]
        kept, piece = pl.ds(COARSE, COARSE) if p == 0 else pl.ds(0, GRID), pl.ds(q * 8, 8)
        return pltpu.make_async_remote_copy(
            src_ref=own.at[h, q, kept],
            dst_ref=new.at[0, kept, piece, pl.ds(h * LANES, LANES)],
            send_sem=n_send.at[p], recv_sem=n_recv.at[p], device_id=(after, g), device_id_type=MESH,
        )

    def modes_of(p):
        h, q = pieces[p]
        here = own.at[h, q]

        def invert(j, carry):
            lam = eigen(h, q, 2 * j)
            inverse[0, j] = 1.0 / (1.0 + 0.5 * lam)
            inverse[1, j] = 1.0 / (1.0 + lam)
            return carry

        lax.fori_loop(0, 4, invert, 0)
        with jax.named_scope(f"ph_wait_r{p}"):
            pltpu.make_async_copy(here, here, r_recv.at[p]).wait()

        def body(j, carry):
            in_modes(h, q, 2 * j, p == 0)
            return carry

        with jax.named_scope(f"ph_modes{p}"):
            lax.fori_loop(0, 4, body, 0)
        if p + 2 < len(pieces):
            send_react(p + 2, 0, BLOCK)
        for k in OFFSETS[:-1]:
            to = partner(k)
            pltpu.make_async_remote_copy(
                src_ref=rim_out.at[h, q, to],
                dst_ref=rim.at[h, g, q],
                send_sem=b_send, recv_sem=b_recv.at[h], device_id=(t, to), device_id_type=MESH,
            ).start()
        pltpu.make_async_copy(rim_out.at[h, q, g], rim.at[h, g, q], b_recv.at[h]).start()
        hand_on(p).start()
        if p == 0:
            for k in range(1, SLICES):
                to = lax.rem(t + k, SLICES)
                pltpu.make_async_remote_copy(
                    src_ref=low.at[to], dst_ref=low_in.at[after], send_sem=l_send, recv_sem=l_recv,
                    device_id=(to, g), device_id_type=MESH,
                ).start()
            pltpu.make_async_copy(low.at[t], low_in.at[after], l_recv).start()

    def nodes_on(h, z):
        return jnp.concatenate(
            [
                base[n, h, z]
                + phi[n, h, z] * whole(rim[h, :, :, n, 0])
                + phi[n, h, BLOCK - 1 - z] * whole(rim[h, :, :, n, 1])
                for n in range(2)
            ],
            axis=1,
        )

    def early(j, carry):
        for z in (2 * j, 2 * j + 1):
            for n, half in enumerate(halves(table_times(per[...], nodes_on(0, z)))):
                base[n, 0, z] = half
        return carry

    mix_rows = mix_out.reshape(COARSE * BLOCK, LANES)

    def node_planes(j, carry):
        planes = (2 * j, 2 * j + 1)
        values = [halves(table_times(per[...], nodes_on(1, z))) for z in planes]
        values = [
            [jnp.concatenate([base[n, 0, z], value[n]], axis=1) for n in range(2)]
            for z, value in zip(planes, values)
        ]
        values = [[reaction(times_table(node, fan[...])) for node in value] for value in values]
        values = [table_times(nat[:COARSE, :], 4.0 * value[0] + value[1]) for value in values]
        value = times_table(jnp.concatenate(values, axis=0), fan[:, :COARSE])
        for i, z in enumerate(planes):
            mix_rows[pl.ds(z, COARSE, stride=BLOCK), :] = value[i * COARSE : (i + 1) * COARSE]
        return carry

    def rim_arrived(h):
        with jax.named_scope(f"ph_wait_rim{h}"):
            pltpu.make_async_copy(rim.at[h], rim.at[h], b_recv.at[h]).wait()

    modes_of(0)
    modes_of(1)
    modes_of(2)
    modes_of(3)
    rim_arrived(0)
    with jax.named_scope("ph_early"):
        lax.fori_loop(0, BLOCK // 2, early, 0)
    rim_arrived(1)

    def mix_source(to_t, to_g, planes):
        return mix_out.at[to_g * HALF + to_t, planes]

    def mix_place(start, count):
        return mix.at[after, pl.ds(pl.multiple_of(own_rows + start, STEP), count)]

    def send_mix(start, count, to_t, k):
        to_g = partner(k)
        pltpu.make_async_remote_copy(
            src_ref=mix_source(to_t, to_g, pl.ds(start, count)), dst_ref=mix_place(start, count),
            send_sem=m_send, recv_sem=m_recv, device_id=(to_t, to_g), device_id_type=MESH,
        ).start()

    def send_rows(start, count, first, last):
        def body(i, carry):
            to_t = lax.rem(t + 4 + (i + 1) // 2 * (1 - 2 * (i % 2)), SLICES)
            for k in OFFSETS[:-1]:
                send_mix(start, count, to_t, k)
            return carry

        lax.fori_loop(first, last, body, 0)

    def send_column(start, count):
        pltpu.make_async_copy(mix_source(t, g, pl.ds(start, count)), mix_place(start, count), m_recv).start()
        for i in FAR_FIRST:
            send_mix(start, count, others[i], 0)

    with jax.named_scope("ph_node0"):
        lax.fori_loop(0, 4, node_planes, 0)
    pl.semaphore_wait(ready, SLICES - 1)
    send_rows(0, 8, 0, SLICES)
    send_column(0, 8)

    def node_round(r, carry):
        lax.fori_loop(4 + 2 * r, 6 + 2 * r, node_planes, 0)
        start = pl.multiple_of(8 + STEP * r, STEP)
        send_rows(start, STEP, 0, SLICES)
        send_column(start, STEP)
        return carry

    with jax.named_scope("ph_node1"):
        lax.fori_loop(0, 2, node_round, 0)
    with jax.named_scope("ph_wait_mix"):
        pltpu.make_async_copy(low_in, low_in, l_recv).wait()
        pltpu.make_async_copy(mix, mix, m_recv).wait()

    with jax.named_scope("ph_scan"):
        decay = 1.0 / (1.0 + (col_c[...] + (row_c[:1, :] + scal_c[g * HALF + t])))
        current = None
        for i in range(SLICES // 2):
            value = table_times(nat[:COARSE, :], jnp.concatenate([mix[2 * i], mix[2 * i + 1]], axis=1))
            for n, half in zip((2 * i, 2 * i + 1), halves(value)):
                gain = low_in[n] + (FACTOR / 6.0) * half
                current = decay * (gain if current is None else current + gain)
                ends[n] = current
    for k in FAR_FIRST:
        to = others[k]
        pltpu.make_async_remote_copy(
            src_ref=ends.at[to], dst_ref=coarse_own.at[t], send_sem=e_send, recv_sem=e_recv,
            device_id=(to, g), device_id_type=MESH,
        ).start()
    pltpu.make_async_copy(ends.at[t], coarse_own.at[t], e_recv).start()
    with jax.named_scope("ph_wait_e"):
        pltpu.make_async_copy(coarse_own, coarse_own, e_recv).wait()

    coarse_rows = coarse.reshape(COARSE * HALF, LANES)
    low_rows = low_out.reshape(COARSE * HALF, LANES)
    for j in range(HALF):
        coarse_rows[pl.ds(j, COARSE, stride=HALF), :] = coarse_own[j]
        low_rows[pl.ds(j, COARSE, stride=HALF), :] = coarse_own[j] * (1.0 / FACTOR)
    new[0, :COARSE, :HALF, :LANES] = low_out[...]

    def sent(ref, sem):
        pltpu.make_async_copy(ref, ref, sem).wait()

    with jax.named_scope("ph_drain"):
        sent(spread.at[:, :, pl.ds(0, GROUPS - 1)], in_send)
        sent(react.at[:, :, pl.ds(0, GROUPS - 1)], r_send)
        sent(rim_out.at[:, :, pl.ds(0, GROUPS - 1)], b_send)
        sent(low.at[pl.ds(0, SLICES - 1)], l_send)
        sent(mix_out.at[pl.ds(0, COARSE - 1)], m_send)
        sent(ends.at[pl.ds(0, SLICES - 1)], e_send)
        for p in range(len(pieces)):
            hand_on(p).wait()


def solution(mesh):
    vmem = pl.BlockSpec(memory_space=pltpu.VMEM)
    hbm = pl.BlockSpec(memory_space=pl.ANY)
    smem = pl.BlockSpec(memory_space=pltpu.SMEM)
    held = tables()

    def per_device(end_modes, initial_modes):
        slab = (2, BLOCK, GRID, LANES)
        coarse = (COARSE, HALF, LANES)
        share = (SLICES, COARSE, LANES)
        dma = pltpu.SemaphoreType.DMA
        scratch = [
            (2, GRID, BLOCK, LANES), (2, ROUNDS, GROUPS, STEP, BLOCK, LANES), (2, GROUPS, BLOCK, BLOCK, LANES),
            (2, 2, GROUPS, BLOCK, 8, LANES), (2, 2, GRID, 8, LANES), (2, *slab), (2, *slab),
            (2, 2, GROUPS, 2, 2, 8, LANES), (2, GROUPS, 2, 2, 2, 8, LANES),
            (COARSE, BLOCK, LANES), (SLICES, GRID, LANES), share, share, share, share, coarse, (2, 4, GRID, GRID),
        ]
        counts = [2, 0, ROUNDS, 0, 4, 0, 2, 4, 4, 0, 0, 0, 0, 0, 0]
        sems = [dma((n,)) if n else dma for n in counts] + [pltpu.SemaphoreType.REGULAR]
        return pl.pallas_call(
            kernel,
            name="pfasst",
            out_shape=(
                pltpu.VMEM(end_modes.shape, F32),
                pltpu.VMEM((1, *coarse), F32),
            ),
            in_specs=[hbm, hbm] + [vmem] * 12 + [smem] * 2,
            out_specs=(vmem, vmem),
            scratch_shapes=[pltpu.VMEM(s, F32) for s in scratch] + sems,
            compiler_params=pltpu.CompilerParams(collective_id=0, has_side_effects=True, vmem_limit_bytes=54 << 20),
        )(end_modes, initial_modes, *held.values())

    return jax.shard_map(
        per_device,
        mesh=mesh,
        in_specs=(P("tm", None, "gx", None), P(None, "gx", None)),
        out_specs=(P("tm", None, "gx", None), P("tm", None, "gx", None)),
        check_vma=False,
    )
```
